32 devices in a mesh: groups: 2 (over y), seq: 4 (over z), batch: 2 (over x), sub: 2 (over core).
Axes of the slice: x: 2, y: 2, z: 4, core: 2. Of those that a mesh axis runs over, the one named last changes fastest.
Arguments:
- gen_hidden: bfloat16 [4, 256, 8192], P(('groups', 'batch'), None, ('seq', 'sub')), parts along dimension 0, may hold values from -6 to 6
- out_proj: bfloat16 [8192, 4096], P(('seq', 'sub')), may hold values from -0.0625 to 0.0625
- norm_gain: bfloat16 [4096], replicated, may hold values from 0.099609375 to 1.8984375
- q_weight: bfloat16 [4096, 4096], P(None, ('seq', 'sub')), may hold values from -0.09375 to 0.09375
- kv_weight: bfloat16 [2, 4096, 1024], P(None, None, ('seq', 'sub')), may hold values from -0.09375 to 0.09375
- kv_cache: bfloat16 [2, 4, 8192, 1024], P(None, ('groups', 'batch'), ('seq', 'sub')), parts along dimension 1, may hold values from -96 to 96
- lengths: int32 [4], P(('groups', 'batch')), parts along dimension 0, may hold values from 1024 to 8192, as said below
- span_start: int32 [4], P(('groups', 'batch')), parts along dimension 0, may hold values from 1024 to 16383, as said below
Outputs:
- attention: bfloat16 [4, 256, 4096], P(('groups', 'batch'), ('seq', 'sub')), parts along dimension 0
The draws below stay inside these ranges and needn't reach their ends.
There are 2 independent parts, one for each index of `groups`. The reference program is written for one: setup_inputs(seed, part) draws one part's arguments, and reference() takes and returns one part's arrays. A program takes and returns all parts, laid end to end along the dimension named above; an argument that names none is the same for every part. Nothing has to cross between parts.
Inputs may be any that keep to these rules, and one draw needn't show every extreme that they name: `lengths`: slots at or past a session's length are not attended. In every draw some session has the full 8192 slots. `span_start`: A session's span starts at or after its window length and less than 8192 later.
All inputs are finite; a program needn't handle non-finite values.
Results may differ from the reference program's by a relative error of at most 0.04.
Values may be sent and summed in bfloat16 or wider, within the bound.
A program may use at most 128 MiB of HBM per device.

```python
import math
import jax
import jax.numpy as jnp
from jax import lax

D_GEN = 8192
D = 4096
QH = 32
KVH = 8
HD = 128
C = 256
WIN = 8192
SESS = 2


def window_draws(key):
    length_key = jax.random.fold_in(key, 101)
    order_key = jax.random.fold_in(key, 202)
    offset_key = jax.random.fold_in(key, 303)
    lengths = jax.random.randint(length_key, (SESS,), WIN // 8, WIN + 1)
    fullest = jax.random.randint(order_key, (), 0, SESS)
    offsets = jax.random.randint(offset_key, (SESS,), 0, WIN)
    picked = jnp.arange(SESS) == fullest
    lengths = jnp.where(picked, WIN, lengths)
    offsets = jnp.where(picked, WIN - 1, offsets)
    starts = lengths + offsets
    return (lengths.astype(jnp.int32), starts.astype(jnp.int32))


def draw_lengths(key, part):
    return window_draws(key)[0]


def draw_span_start(key, part):
    return window_draws(key)[1]


def draw_kv_cache(key, part):
    shape = (2, SESS, WIN, KVH * HD)
    values = jnp.clip(jax.random.normal(jax.random.fold_in(key, 1), shape, jnp.float32), -6.0, 6.0)
    return values.astype(jnp.bfloat16)


def with_spikes(entries, rng, source, target, shards_of, factor):
    def block_of(axis_at):
        return (jnp.arange(entries.shape[axis_at]) // (entries.shape[axis_at] // shards_of)).reshape((-1,) + (1,) * (entries.ndim - 1 - axis_at))

    near = jax.random.permutation(rng, shards_of)[block_of(target)]
    far = (block_of(target) + shards_of // 2) % shards_of
    return jnp.where((block_of(source) == near) | (block_of(source) == far), factor * entries, entries)


def levels(own_key, dims, cuts, smallest, high):
    def one(dim, parts):
        steps = jax.random.uniform(jax.random.fold_in(jax.random.fold_in(own_key, 6), dim), (parts,), jnp.float32, smallest / len(cuts), high / len(cuts))
        return jnp.repeat(jnp.exp(steps), dims[dim] // parts).reshape((-1,) + (1,) * (len(dims) - dim - 1))

    gain = one(*cuts[0])
    for cut in cuts[1:]:
        gain = gain * one(*cut)
    return gain


def gaussian(stream_key, extent, scale, limit, pieces=(), kind=jnp.bfloat16):
    array = scale * jax.random.normal(stream_key, extent, jnp.float32)
    if pieces:
        array = array * levels(stream_key, extent, pieces, -0.22, 0.18)
    return jnp.clip(array, -limit, limit).astype(kind)


def noise_with(key, shape, deviation, bound, shards, heavy, held_as=jnp.bfloat16):
    values = deviation * jax.random.normal(key, shape, jnp.float32)
    if shards:
        values = values * levels(key, shape, shards, -0.22, 0.18)
    return jnp.clip(with_spikes(values, jax.random.fold_in(key, 3), *heavy), -bound, bound).astype(held_as)


def setup_inputs(seed: int = 0, part: int = 0) -> dict:
    streams_of = jax.random.split(jax.random.key(seed), 9)
    own_keys = jax.random.split(jax.random.fold_in(streams_of[8], part), 9)
    gen_hidden = noise_with(own_keys[0], (SESS, C, D_GEN), 1.0, 6.0, ((0, 2), (2, 8)), (2, 1, 8, 2.0))
    out_proj = gaussian(streams_of[1], (D_GEN, D), D_GEN ** -0.5, 0.0625, ((0, 8),))
    norm_gain = jnp.clip(1.0 + 0.18 * jax.random.normal(streams_of[2], (D,), jnp.float32), 0.099609375, 1.8984375).astype(jnp.bfloat16)
    q_weight = gaussian(streams_of[3], (D, QH * HD), D ** -0.5, 0.09375, ((1, 8),))
    kv_weight = gaussian(streams_of[4], (2, D, KVH * HD), D ** -0.5, 0.09375, ((2, 8),))
    kv_cache = draw_kv_cache(jax.random.fold_in(jax.random.fold_in(streams_of[8], part), 71), part)
    lengths = draw_lengths(jax.random.fold_in(jax.random.fold_in(streams_of[8], part), 71), part)
    span_start = draw_span_start(jax.random.fold_in(jax.random.fold_in(streams_of[8], part), 71), part)
    return {"gen_hidden": gen_hidden, "out_proj": out_proj, "norm_gain": norm_gain, "q_weight": q_weight, "kv_weight": kv_weight, "kv_cache": kv_cache, "lengths": lengths, "span_start": span_start}


EPS = 1e-05
THETA = 500000.0
NEG = -1e+30

def rotate(values, positions):
    half = values.shape[-1] // 2
    freq = THETA ** (-jnp.arange(half, dtype=jnp.float32) * 2.0 / values.shape[-1])
    angle = positions.astype(jnp.float32)[..., None] * freq
    cosine = jnp.cos(angle)[..., None, :]
    sine = jnp.sin(angle)[..., None, :]
    first = values[..., :half]
    second = values[..., half:]
    return jnp.concatenate([first * cosine - second * sine, second * cosine + first * sine], axis=-1)

def reference(gen_hidden, out_proj, norm_gain, q_weight, kv_weight, kv_cache, lengths, span_start):
    group = QH // KVH
    scale = 1.0 / math.sqrt(HD)

    def one_session(items):
        hidden, cache_keys, cache_values, length, start = items
        inputs = jnp.dot(hidden, out_proj, preferred_element_type=jnp.float32).astype(jnp.bfloat16)
        wide = inputs.astype(jnp.float32)
        inverse = lax.rsqrt(lax.optimization_barrier(jnp.mean(wide * wide, axis=-1, keepdims=True)) + EPS)
        normed = (wide * inverse * norm_gain.astype(jnp.float32)).astype(jnp.bfloat16)
        positions = start + jnp.arange(C, dtype=jnp.int32)
        query = jnp.dot(normed, q_weight, preferred_element_type=jnp.float32).reshape(C, QH, HD)
        query = rotate(query, positions).astype(jnp.bfloat16)
        key_raw = jnp.dot(normed, kv_weight[0], preferred_element_type=jnp.float32).astype(jnp.bfloat16)
        key_raw = lax.optimization_barrier(key_raw)
        new_keys = rotate(key_raw.astype(jnp.float32).reshape(C, KVH, HD), positions).astype(jnp.bfloat16)
        new_values = jnp.dot(normed, kv_weight[1], preferred_element_type=jnp.float32).astype(jnp.bfloat16)
        keys = jnp.concatenate([cache_keys.reshape(WIN, KVH, HD), new_keys], axis=0).astype(jnp.float32)
        values = jnp.concatenate([cache_values.reshape(WIN, KVH, HD), new_values.reshape(C, KVH, HD)], axis=0).astype(jnp.float32)
        grouped = query.reshape(C, KVH, group, HD).astype(jnp.float32)
        scores = jnp.einsum('cagh,wah->agcw', grouped, keys) * scale
        live_cache = jnp.broadcast_to(jnp.arange(WIN, dtype=jnp.int32)[None, :] < length, (C, WIN))
        causal = jnp.arange(C, dtype=jnp.int32)[None, :] <= jnp.arange(C, dtype=jnp.int32)[:, None]
        live = jnp.concatenate([live_cache, causal], axis=1)
        scores = jnp.where(live, scores, NEG)
        top = lax.optimization_barrier(jnp.max(scores, axis=-1, keepdims=True))
        weights = jnp.exp(scores - top)
        total = lax.optimization_barrier(jnp.sum(weights, axis=-1))
        probs = lax.optimization_barrier(weights.astype(jnp.bfloat16))
        mixed = jnp.einsum('agcw,wah->cagh', probs.astype(jnp.float32), values)
        result = mixed / jnp.transpose(total, (2, 0, 1))[..., None]
        return result.astype(jnp.bfloat16).reshape(C, QH * HD)
    return lax.map(one_session, (gen_hidden, kv_cache[0], kv_cache[1], lengths, span_start))
```

```python
import functools
import math

import jax
import jax.numpy as jnp
import numpy as np
from jax import lax
from jax.experimental import pallas as pl
from jax.experimental.pallas import tpu as pltpu
from jax.sharding import PartitionSpec as P

QH = 32
KVH = 8
HD = 128


EPS = 1e-05
THETA = 500000.0
NEG = -1e30


def rotate(values, positions):
    half = values.shape[-1] // 2
    freq = THETA ** (-jnp.arange(half, dtype=jnp.float32) * 2.0 / values.shape[-1])
    angle = positions.astype(jnp.float32)[..., None] * freq
    cosine = jnp.cos(angle)[..., None, :]
    sine = jnp.sin(angle)[..., None, :]
    first = values[..., :half]
    second = values[..., half:]
    return jnp.concatenate(
        [first * cosine - second * sine, second * cosine + first * sine], axis=-1
    )


def body(gen_hidden, out_proj, norm_gain, q_weight, kv_weight, kv_cache, lengths, span_start):
    sessions, span, _ = gen_hidden.shape
    shards = lax.axis_size(("seq", "sub"))
    mine = lax.axis_index(("seq", "sub"))
    rows = span // shards
    local_heads = q_weight.shape[1] // HD
    group = QH // KVH
    scale = 1.0 / math.sqrt(HD)
    window_local = kv_cache.shape[2]
    summed = lax.psum(
        jnp.einsum("sci,id->csd", gen_hidden, out_proj, preferred_element_type=jnp.float32),
        ("seq", "sub"),
    )
    inputs = summed.astype(jnp.bfloat16)
    wide = inputs.astype(jnp.float32)
    inverse = lax.rsqrt(jnp.mean(wide * wide, axis=-1, keepdims=True) + EPS)
    normed = (wide * inverse * norm_gain.astype(jnp.float32)).astype(jnp.bfloat16)
    positions = span_start[None, :] + jnp.arange(span, dtype=jnp.int32)[:, None]
    query = jnp.einsum("csd,dh->csh", normed, q_weight, preferred_element_type=jnp.float32)
    query = rotate(query.reshape(span, sessions, local_heads, HD), positions).astype(jnp.bfloat16)
    kv_raw = jnp.einsum(
        "csd,jdk->jcsk", normed, kv_weight, preferred_element_type=jnp.float32
    ).astype(jnp.bfloat16)
    query_rows = jnp.arange(span, dtype=jnp.int32)
    new_rows = lax.all_to_all(kv_raw, ("seq", "sub"), split_axis=1, concat_axis=3, tiled=True)
    my_positions = lax.dynamic_slice_in_dim(positions, mine * rows, rows, 0)
    new_keys = rotate(
        new_rows[0].reshape(rows, sessions, KVH, HD).astype(jnp.float32), my_positions
    ).astype(jnp.bfloat16)
    new_values = new_rows[1].reshape(rows, sessions, KVH, HD)
    every_query = lax.all_gather(
        query.reshape(span, sessions, local_heads * HD), ("seq", "sub"), axis=2, tiled=True
    )
    grouped = every_query.reshape(span, sessions, KVH, group, HD)
    cached = kv_cache.reshape(2, sessions, window_local, KVH, HD)
    cache_scores = (
        jnp.einsum("csagh,swah->sagcw", grouped, cached[0], preferred_element_type=jnp.float32)
        * scale
    )
    slots = mine * window_local + jnp.arange(window_local, dtype=jnp.int32)
    live = slots[None, :] < lengths[:, None]
    cache_scores = jnp.where(live[:, None, None, None, :], cache_scores, NEG)
    span_scores = (
        jnp.einsum("csagh,tsah->sagct", grouped, new_keys, preferred_element_type=jnp.float32)
        * scale
    )
    key_rows = mine * rows + jnp.arange(rows, dtype=jnp.int32)
    causal = key_rows[None, :] <= query_rows[:, None]
    span_scores = jnp.where(causal, span_scores, NEG)
    top = jnp.maximum(jnp.max(cache_scores, axis=-1), jnp.max(span_scores, axis=-1))
    cache_weights = jnp.exp(cache_scores - top[..., None])
    span_weights = jnp.exp(span_scores - top[..., None])
    total = jnp.sum(cache_weights, axis=-1) + jnp.sum(span_weights, axis=-1)
    mixed = jnp.einsum(
        "sagcw,swah->scagh",
        cache_weights.astype(jnp.bfloat16),
        cached[1],
        preferred_element_type=jnp.float32,
    )
    mixed = mixed + jnp.einsum(
        "sagct,tsah->scagh",
        span_weights.astype(jnp.bfloat16),
        new_values,
        preferred_element_type=jnp.float32,
    )
    partial_value = mixed.reshape(1, sessions, span, QH * HD)
    peak = jnp.transpose(top, (0, 3, 1, 2)).reshape(1, sessions, span, QH)
    mass = jnp.transpose(total, (0, 3, 1, 2)).reshape(1, sessions, span, QH)
    pieces, peaks, masses = (
        lax.all_to_all(
            partial_value.astype(jnp.bfloat16),
            ("seq", "sub"),
            split_axis=2,
            concat_axis=0,
            tiled=True,
        ).astype(partial_value.dtype),
        lax.all_to_all(
            peak.astype(jnp.bfloat16), ("seq", "sub"), split_axis=2, concat_axis=0, tiled=True
        ).astype(peak.dtype),
        lax.all_to_all(
            mass.astype(jnp.bfloat16), ("seq", "sub"), split_axis=2, concat_axis=0, tiled=True
        ).astype(mass.dtype),
    )
    best = jnp.max(peaks, axis=0)
    factor = jnp.exp(peaks - best[None])
    numer = jnp.sum(factor[..., None] * pieces.reshape(shards, sessions, rows, QH, HD), axis=0)
    denom = jnp.sum(factor * masses, axis=0)
    return (numer / denom[..., None]).astype(jnp.bfloat16).reshape(sessions, rows, QH * HD)


MESH = pl.DeviceIdType.MESH
BF = jnp.bfloat16
F32 = jnp.float32
TILE = 512
LEFT, FULL, QKV, ATTEND, MERGE, PASS, NEED_W, NEED_KV = range(1, 9)
CHUNKS = 4
ORDER = (0, 3, 2, 1)
PLAN = (
    (
        128, 136, 144, 152, 131, 448, 192, 512, 256, 139, 257, 147, 258, 155, 130, 216,
        281, 138, 146, 154, 208, 129, 282, 273, 137, 145, 153, 200, 280, 272, 322, 274,
        264, 265, 321, 283, 259, 323, 266, 275, 267, 320, 0, 0, 0, 0, 0, 0,
        0, 0, 0, 0, 0, 0, 0, 0, 0, 0, 0, 0, 0, 0, 0, 0,
        0, 0, 0, 0, 0, 0, 0, 0, 0, 0, 0, 0, 0, 0, 0, 0,
        0, 0,
    ),
    (
        64, 72, 80, 128, 88, 136, 67, 144, 75, 152, 83, 131, 448, 192, 91, 66,
        139, 512, 257, 74, 147, 386, 258, 82, 155, 90, 130, 216, 65, 73, 138, 146,
        81, 154, 89, 410, 282, 384, 129, 208, 137, 408, 256, 145, 280, 153, 387, 259,
        200, 400, 402, 281, 322, 323, 345, 346, 273, 321, 411, 337, 283, 394, 272, 403,
        392, 274, 275, 344, 265, 395, 336, 264, 320, 338, 266, 267, 347, 330, 339, 329,
        331, 328,
    ),
    (
        64, 72, 80, 128, 88, 136, 67, 144, 75, 152, 83, 131, 448, 192, 91, 66,
        139, 512, 258, 74, 147, 385, 257, 82, 155, 90, 130, 216, 65, 73, 138, 146,
        81, 154, 89, 409, 281, 387, 129, 208, 137, 259, 145, 322, 323, 153, 321, 384,
        256, 411, 401, 200, 408, 403, 282, 283, 393, 280, 400, 266, 345, 265, 346, 274,
        395, 267, 392, 320, 264, 275, 273, 344, 337, 331, 272, 336, 338, 330, 329, 347,
        328, 339,
    ),
    (
        128, 136, 144, 152, 131, 448, 192, 512, 259, 139, 258, 147, 257, 155, 130, 216,
        282, 138, 146, 154, 208, 129, 281, 274, 137, 145, 153, 200, 256, 275, 273, 267,
        272, 266, 345, 265, 346, 283, 264, 280, 344, 347, 0, 0, 0, 0, 0, 0,
        0, 0, 0, 0, 0, 0, 0, 0, 0, 0, 0, 0, 0, 0, 0, 0,
        0, 0, 0, 0, 0, 0, 0, 0, 0, 0, 0, 0, 0, 0, 0, 0,
        0, 0,
    ),
)


def packed_plan(steps):
    steps = list(steps) + [0] * (-len(steps) % 3)
    return [a + 1024 * b + 1048576 * c for a, b, c in zip(*[iter(steps)] * 3)]


def fused_kernel(
    shards_z,
    hid,
    wo,
    gain,
    wq,
    wkv,
    cache,
    lengths,
    starts,
    freqs,
    out,
    hid_v,
    wo_v,
    w_v,
    k_v,
    v_v,
    p_send,
    p_recv,
    own_part,
    part,
    part_in,
    side,
    side_in,
    x_all,
    xg_v,
    q_all,
    kn,
    vn,
    o_loc,
    o_in,
    f_recv,
    rope_v,
    in_sem,
    wo_sem,
    kvl_sem,
    kvs_sem,
    kvr_sem,
    ps_sem,
    pr_sem,
    outs_sem,
    outr_sem,
    mids_sem,
    midr_sem,
    xs_sem,
    xr_sem,
    fws_sem,
    fwr_sem,
    qs_sem,
    qr_sem,
    os_sem,
    or_sem,
    fs_sem,
    fr_sem,
):
    Z = shards_z
    z = lax.axis_index("seq")
    c = lax.axis_index("sub")
    other = 1 - c
    rows = hid.shape[2]
    pair = 2 * rows
    span = Z * pair
    width = wo.shape[1]
    cw = width // CHUNKS
    ql = wq.shape[1]
    heads = ql // HD
    stack = heads * pair
    wl = cache.shape[1]

    inner = (z == 1) | (z == 2)
    outer = jnp.logical_not(inner)
    near = z + 1 - 2 * lax.rem(z, 2)
    far_in = jnp.where(z < 2, 2, 1)

    def remote(src, dst, ss, rs, zz, cc):
        return pltpu.make_async_remote_copy(
            src_ref=src,
            dst_ref=dst,
            send_sem=ss,
            recv_sem=rs,
            device_id={"seq": zz, "sub": cc},
            device_id_type=MESH,
        )

    def hid_copy():
        return (
            pltpu.make_async_copy(hid.at[:, other], hid_v.at[0], in_sem.at[0]),
            pltpu.make_async_copy(hid.at[:, c], hid_v.at[1], in_sem.at[4]),
        )

    def wo_copy(k):
        return pltpu.make_async_copy(
            wo.at[:, pl.ds(pl.multiple_of(k * cw, cw), cw)], wo_v.at[k], wo_sem.at[k]
        )

    def w_copies():
        return (
            pltpu.make_async_copy(wq, w_v.at[:, 0:ql], in_sem.at[1]),
            pltpu.make_async_copy(wkv.at[0], w_v.at[:, ql : ql + HD], in_sem.at[2]),
            pltpu.make_async_copy(wkv.at[1], w_v.at[:, ql + HD : ql + 2 * HD], in_sem.at[3]),
        )

    def kv_src(i, j, cc):
        return cache.at[i, :, pl.ds(pl.multiple_of((2 * j + cc) * HD, HD), HD)]

    def kv_dst(i, j):
        return (k_v, v_v)[i].at[j, pl.ds(pl.multiple_of(c * wl, wl), wl), :]

    def kv_local(i, j):
        return pltpu.make_async_copy(kv_src(i, j, c), kv_dst(i, j), kvl_sem.at[i, j])

    def kv_remote(i, j):
        return remote(
            kv_src(i, j, other), kv_dst(i, j), kvs_sem.at[i, j], kvr_sem.at[i, j], z, other
        )

    def pair_copy(k):
        return remote(p_send.at[k], p_recv.at[k], ps_sem.at[k], pr_sem.at[k], z, other)

    def out_copy(k, r):
        return remote(part.at[k, r], part_in.at[k, r], outs_sem.at[k, r], outr_sem.at[k, r], near, c)

    def mid_copy(k, r):
        return remote(
            side.at[k, r], side_in.at[k, r], mids_sem.at[k, r], midr_sem.at[k, r], far_in, c
        )

    def x_copy(k, r):
        blk = x_all.at[k, 2 * r + c]
        return remote(blk, blk, xs_sem.at[k, r], xr_sem.at[k, r], near, c)

    def fw_copy(k, r, core):
        blk = x_all.at[k, 2 * r + core]
        return remote(blk, blk, fws_sem.at[k, r], fwr_sem.at[k, r], z, other)

    def q_copy(r, j, sem, who):
        blk = q_all.at[r, j]
        return remote(blk, blk, qs_sem.at[r, sem], qr_sem.at[r, j], who, c)

    def o_copy(r, j):
        up = jnp.where(z < r, 0, 1)
        who = jnp.where(z < r, z + 1, z - 1)
        return remote(
            o_loc.at[r, j], o_in.at[r, j, up], os_sem.at[r, j], or_sem.at[r, j, up], who, c
        )

    def f_copy(j):
        src = o_loc.at[z, j, 0:heads, pl.ds(pl.multiple_of(other * rows, rows), rows), :]
        return remote(src, f_recv.at[j], fs_sem.at[j], fr_sem.at[j], z, other)

    for copy in hid_copy():
        copy.start()
    for k in range(CHUNKS):
        wo_copy(k).start()
    barrier = pltpu.get_barrier_semaphore()
    pl.semaphore_signal(barrier, inc=1, device_id={"seq": near, "sub": c}, device_id_type=MESH)
    pl.semaphore_signal(barrier, inc=1, device_id={"seq": z, "sub": other}, device_id_type=MESH)

    @pl.when(inner)
    def _():
        pl.semaphore_signal(
            barrier, inc=1, device_id={"seq": far_in, "sub": c}, device_id_type=MESH
        )

    words = [
        jnp.where(z < 2, jnp.where(z == 0, w[0], w[1]), jnp.where(z == 2, w[2], w[3]))
        for w in zip(*(packed_plan(steps) for steps in PLAN))
    ]

    def step_at(n):
        at = lax.div(n, 3)
        level = words
        bit = 1
        while len(level) > 1:
            odd = lax.rem(lax.div(at, bit), 2) == 1
            level = [
                jnp.where(odd, level[i + 1], level[i]) if i + 1 < len(level) else level[i]
                for i in range(0, len(level), 2)
            ]
            bit *= 2
        word = level[0]
        which = lax.rem(n, 3)
        word = jnp.where(
            which == 0, word, jnp.where(which == 1, lax.div(word, 1024), lax.div(word, 1048576))
        )
        return lax.rem(word, 1024)

    kn[...] = jnp.zeros_like(kn)
    vn[...] = jnp.zeros_like(vn)

    pl.semaphore_wait(barrier, jnp.where(inner, 3, 2))

    for copy in hid_copy():
        copy.wait()

    def pair_sum(k):
        pair_copy(k).wait_recv()
        both = own_part[k] + p_recv[k].astype(F32)
        part[k] = both.astype(BF).reshape(Z, rows, cw)

        @pl.when(outer)
        def _():
            out_copy(k, ORDER[0]).start()

    def stage_a(k, carry):
        wo_copy(k).wait()
        lhs = hid_v[...].reshape(span, hid.shape[3])
        half = Z * rows

        def go(t, carry):
            cols = pl.ds(pl.multiple_of(t * TILE, TILE), TILE)
            value = jnp.dot(lhs, wo_v[k, :, cols], preferred_element_type=F32)
            p_send[k, :, cols] = value[:half].astype(BF)
            own_part[k, :, cols] = value[half:]
            return carry

        lax.fori_loop(0, cw // TILE, go, 0)
        pair_copy(k).start()

        @pl.when(k >= 1)
        def _():
            pair_sum(k - 1)

        return carry

    lax.fori_loop(0, CHUNKS, stage_a, 0)
    for copy in w_copies():
        copy.start()
    pair_sum(CHUNKS - 1)

    @pl.when(outer)
    def _():
        for r in ORDER[1:]:
            for k in range(CHUNKS):
                out_copy(k, r).start()

    for i in range(2):
        for j in range(Z):
            kv_local(i, j).start()
            kv_remote(i, j).start()

    angle = (starts[0] + lax.broadcasted_iota(jnp.int32, (span, HD), 0)).astype(F32) * freqs[...]
    rope_v[0] = jnp.cos(angle)
    sines = jnp.sin(angle)
    first = lax.broadcasted_iota(jnp.int32, (span, HD), 1) < HD // 2
    rope_v[1] = jnp.where(first, -sines, sines)

    length = lengths[0]
    slots = z * 2 * wl + lax.broadcasted_iota(jnp.int32, (1, 2 * wl), 1)
    live = slots < length
    c2 = math.log2(math.e) / math.sqrt(HD)
    nt = (((1,), (1,)), ((), ()))
    lane = lax.broadcasted_iota(jnp.int32, (pair, HD), 1)

    def add_near(k, r):
        out_copy(k, r).wait_recv()
        both = part[k, r].astype(F32) + part_in[k, r].astype(F32)
        side[k, r] = both.astype(BF)
        mid_copy(k, r).start()

    def add_far(k, r):
        @pl.when(inner)
        def _():
            mid_copy(k, r).wait_recv()
            both = side[k, r].astype(F32) + side_in[k, r].astype(F32)
            x_all[k, 2 * r + c] = both.astype(BF)
            x_copy(k, r).start()

        @pl.when(outer)
        def _():
            x_copy(k, r).wait_recv()

        fw_copy(k, r, c).start()

    def project(r):
        squares = jnp.zeros((pair, 1), F32)
        for k in range(CHUNKS):
            fw_copy(k, r, other).wait_recv()
            x = x_all[k, pl.ds(2 * r, 2)].reshape(pair, cw).astype(F32)
            squares = squares + jnp.sum(x * x, axis=-1, keepdims=True)
            cols = slice(k * cw, (k + 1) * cw)
            xg_v[:, cols] = (x * gain[cols].astype(F32).reshape(1, cw)).astype(BF)
        inverse = lax.rsqrt(squares * (1.0 / width) + EPS)
        acc = jnp.dot(xg_v[...], w_v[...], preferred_element_type=F32)
        at = pl.ds(pl.multiple_of(r * pair, pair), pair)
        cosine = rope_v[0, at, :]
        sine = rope_v[1, at, :]

        def rope(value):
            return value * cosine + pltpu.roll(value, HD // 2, 1) * sine

        for h in range(heads):
            value = acc[:, h * HD : (h + 1) * HD] * inverse
            q_all[r, z, h] = (rope(value) * c2).astype(BF)
        q_copy(r, z, 0, near).start()

        @pl.when(inner)
        def _():
            q_copy(r, z, 1, far_in).start()

        key_raw = (acc[:, ql : ql + HD] * inverse).astype(BF)
        kn[at, :] = rope(key_raw.astype(F32)).astype(BF)
        vn[at, :] = (acc[:, ql + HD : ql + 2 * HD] * inverse).astype(BF)

    def stats_of(lse):
        stats = jnp.zeros((pair, HD), F32)
        for h in range(heads):
            stats = jnp.where(
                (lane == h) | (lane == h + heads), lse[h * pair : (h + 1) * pair], stats
            )
        return stats

    def packed(stats):
        high = stats.astype(BF).astype(F32)
        return jnp.where(lane < heads, high, stats - high).astype(BF)

    def unpacked(block):
        both = block.astype(F32)
        return both + pltpu.roll(both, HD - heads, 1)

    def blend(r, j, part_of, stats):
        mine = unpacked(o_loc[r, j, heads])
        best = jnp.maximum(mine, stats)
        a = jnp.exp2(mine - best)
        b = jnp.exp2(stats - best)
        total = a + b
        inv = 1.0 / total
        a = a * inv
        b = b * inv
        for h in range(heads):
            mix = a[:, h : h + 1] * o_loc[r, j, h].astype(F32) + b[:, h : h + 1] * part_of(h)
            o_loc[r, j, h] = mix.astype(BF)
        lse = best + jnp.log2(total)
        lse = jnp.where(lane < heads, lse, pltpu.roll(lse, heads, 1))
        o_loc[r, j, heads] = packed(lse)

    def softmaxed(s, values):
        top = jnp.max(s, axis=-1, keepdims=True)
        p = jnp.exp2(s - top)
        total = jnp.sum(p, axis=-1, keepdims=True)
        mixed = jnp.dot(p.astype(BF), values, preferred_element_type=F32)
        return mixed * (1.0 / total), top + jnp.log2(total)

    def attend(r, j):
        @pl.when(outer & (j != z))
        def _():
            q_copy(r, j, 0, near).wait_recv()

        q = q_all[r, j].reshape(stack, HD)
        s = lax.dot_general(q, k_v[j], nt, preferred_element_type=F32)
        s = jnp.where(live, s, NEG)
        mixed, lse = softmaxed(s, v_v[j])
        o_loc[r, j, 0:heads] = mixed.astype(BF).reshape(heads, pair, HD)
        o_loc[r, j, heads] = packed(stats_of(lse))

        @pl.when(j == z)
        def _():
            s2 = lax.dot_general(q_all[r, j].reshape(stack, HD), kn[...], nt, preferred_element_type=F32)
            at = lax.rem(lax.broadcasted_iota(jnp.int32, (stack, span), 0), pair) + r * pair
            t = lax.broadcasted_iota(jnp.int32, (stack, span), 1)
            s2 = jnp.where(t <= at, s2, NEG)
            mixed, lse = softmaxed(s2, vn[...])
            blend(r, j, lambda h: mixed[h * pair : (h + 1) * pair], stats_of(lse))

        @pl.when(outer & (z != r))
        def _():
            o_copy(r, j).start()

    def merge(r, j):
        def one(way, carry):
            has = jnp.where(way == 0, (z >= 1) & (z <= r), (z <= Z - 2) & (z >= r))

            @pl.when(has)
            def _():
                remote(
                    o_loc.at[r, j], o_in.at[r, j, way], os_sem.at[r, j], or_sem.at[r, j, way], near, c
                ).wait_recv()
                blend(
                    r, j, lambda h: o_in[r, j, way, h].astype(F32), unpacked(o_in[r, j, way, heads])
                )

            return carry

        lax.fori_loop(0, 2, one, 0)

        @pl.when(z != r)
        def _():
            o_copy(r, j).start()

        @pl.when(z == r)
        def _():
            f_copy(j).start()
            keep = pl.ds(pl.multiple_of(c * rows, rows), rows)
            for h in range(heads):
                col = pl.ds(pl.multiple_of((2 * j + c) * ql + h * HD, HD), HD)
                out[0, :, col] = o_loc[r, j, h, keep, :]

    def pass_on(r, j):
        q_copy(r, j, 0, near).wait_recv()

        @pl.when(j == near)
        def _():
            q_copy(r, j, 2, far_in).start()

        @pl.when(j != near)
        def _():
            q_copy(r, j, jnp.where(j == far_in, 3, 4), near).start()

    def need_w():
        for copy in w_copies():
            copy.wait()

    def need_kv():
        for i in range(2):
            for j in range(Z):
                kv_local(i, j).wait()
                kv_remote(i, j).wait_recv()

    def run(n, carry):
        step = step_at(n)
        kind = lax.div(step, 64)
        a = lax.rem(lax.div(step, 8), 8)
        b = lax.rem(step, 8)
        for code, what in (
            (LEFT, lambda: add_near(a, b)),
            (FULL, lambda: add_far(a, b)),
            (QKV, lambda: project(a)),
            (ATTEND, lambda: attend(a, b)),
            (MERGE, lambda: merge(a, b)),
            (PASS, lambda: pass_on(a, b)),
            (NEED_W, need_w),
            (NEED_KV, need_kv),
        ):
            pl.when(kind == code)(what)
        return carry

    lax.fori_loop(0, len(PLAN[0]), run, 0)

    for j in range(Z):
        f_copy(j).wait_recv()
        for h in range(heads):
            col = pl.ds(pl.multiple_of((2 * j + other) * ql + h * HD, HD), HD)
            out[0, :, col] = f_recv[j, h]

    for j in range(Z):
        f_copy(j).wait_send()
    for i in range(2):
        for j in range(Z):
            kv_remote(i, j).wait_send()

    def drain(k, carry):
        pair_copy(k).wait_send()
        for r in range(Z):
            fw_copy(k, r, c).wait_send()

            @pl.when(outer)
            def _():
                out_copy(k, r).wait_send()

            @pl.when(inner)
            def _():
                mid_copy(k, r).wait_send()
                x_copy(k, r).wait_send()

        return carry

    lax.fori_loop(0, CHUNKS, drain, 0)

    def drain_q(r, carry):
        q_copy(r, z, 0, near).wait_send()

        @pl.when(inner)
        def _():
            for sem in range(1, 5):
                q_copy(r, z, sem, near).wait_send()

        @pl.when(z != r)
        def _():
            for j in range(Z):
                o_copy(r, j).wait_send()

        return carry

    lax.fori_loop(0, Z, drain_q, 0)


def fused(gen_hidden, out_proj, norm_gain, q_weight, kv_weight, kv_cache, lengths, span_start):
    Z = lax.axis_size("seq")
    _, span, dl = gen_hidden.shape
    rows = span // (2 * Z)
    width = out_proj.shape[1]
    cw = width // CHUNKS
    ql = q_weight.shape[1]
    heads = ql // HD
    wl = kv_cache.shape[2]
    half = HD // 2
    freq = THETA ** (-np.arange(half, dtype=np.float64) * 2.0 / HD)
    freqs = jnp.asarray(np.concatenate([freq, freq])[None, :].astype(np.float32))
    any_spec = pl.BlockSpec(memory_space=pl.ANY)
    vm_spec = pl.BlockSpec(memory_space=pltpu.VMEM)
    sm_spec = pl.BlockSpec(memory_space=pltpu.SMEM)
    dma = pltpu.SemaphoreType.DMA
    V = pltpu.VMEM
    return pl.pallas_call(
        functools.partial(fused_kernel, Z),
        out_shape=jax.ShapeDtypeStruct((1, rows, 2 * Z * ql), BF),
        in_specs=[any_spec, any_spec, vm_spec, any_spec, any_spec, any_spec, sm_spec, sm_spec, vm_spec],
        out_specs=vm_spec,
        scratch_shapes=[
            V((2, Z, rows, dl), BF),
            V((CHUNKS, dl, cw), BF),
            V((width, ql + 2 * HD), BF),
            V((Z, 2 * wl, HD), BF),
            V((Z, 2 * wl, HD), BF),
            V((CHUNKS, Z * rows, cw), BF),
            V((CHUNKS, Z * rows, cw), BF),
            V((CHUNKS, Z * rows, cw), F32),
            V((CHUNKS, Z, rows, cw), BF),
            V((CHUNKS, Z, rows, cw), BF),
            V((CHUNKS, Z, rows, cw), BF),
            V((CHUNKS, Z, rows, cw), BF),
            V((CHUNKS, 2 * Z, rows, cw), BF),
            V((2 * rows, width), BF),
            V((Z, Z, heads, 2 * rows, HD), BF),
            V((span, HD), BF),
            V((span, HD), BF),
            V((Z, Z, heads + 1, 2 * rows, HD), BF),
            V((Z, Z, 2, heads + 1, 2 * rows, HD), BF),
            V((Z, heads, rows, HD), BF),
            V((2, span, HD), F32),
            dma((5,)),
            dma((CHUNKS,)),
            dma((2, Z)),
            dma((2, Z)),
            dma((2, Z)),
            dma((CHUNKS,)),
            dma((CHUNKS,)),
            dma((CHUNKS, Z)),
            dma((CHUNKS, Z)),
            dma((CHUNKS, Z)),
            dma((CHUNKS, Z)),
            dma((CHUNKS, Z)),
            dma((CHUNKS, Z)),
            dma((CHUNKS, Z)),
            dma((CHUNKS, Z)),
            dma((Z, 5)),
            dma((Z, Z)),
            dma((Z, Z)),
            dma((Z, Z, 2)),
            dma((Z,)),
            dma((Z,)),
        ],
        compiler_params=pltpu.CompilerParams(
            collective_id=0, has_side_effects=True, vmem_limit_bytes=64000000
        ),
    )(
        gen_hidden.reshape(Z, 2, rows, dl),
        out_proj,
        norm_gain,
        q_weight,
        kv_weight,
        kv_cache.reshape(2, wl, KVH * HD),
        lengths,
        span_start,
        freqs,
    )


def solution(mesh):
    placed = (
        P(("groups", "batch"), None, ("seq", "sub")),
        P(("seq", "sub"), None),
        P(),
        P(None, ("seq", "sub")),
        P(None, None, ("seq", "sub")),
        P(None, ("groups", "batch"), ("seq", "sub"), None),
        P(("groups", "batch")),
        P(("groups", "batch")),
    )
    aligned = mesh.shape["sub"] == 2 and mesh.shape["seq"] * 2 == KVH
    return jax.shard_map(
        fused if aligned else body,
        mesh=mesh,
        in_specs=placed,
        out_specs=P(("groups", "batch"), ("seq", "sub"), None),
        check_vma=False,
    )
```
